32 devices in a mesh: circ: 8 (over z, x), cell: 4 (over y, core).
Axes of the slice: x: 2, y: 2, z: 4, core: 2. Of those that a mesh axis runs over, the one named last changes fastest.
Arguments:
- flow_state: bfloat16 [35, 8, 16, 1024], P(None, 'circ', 'cell'), may hold values from -6 to 6
- time_coef: float32 [8, 16, 1024], P('circ', 'cell'), may hold values from 0.3 to 3
- axial_damp: bfloat16 [8, 16, 1024], P('circ', 'cell'), may hold values from 0.19921875 to 2
- plane_damp: bfloat16 [8, 16, 2048], P('circ', 'cell'), may hold values from 0.19921875 to 2
- periodic_damp: bfloat16 [8, 16, 64], P('circ', 'cell'), may hold values from 0.19921875 to 2
- flux_jacobian: float32 [3, 5, 5], replicated, may hold values from -2.5 to 2.5
- face_cells: int32 [2, 2048], replicated, may hold values from 0 to 1023, as said below
- periodic_cells: int32 [2, 64], replicated, may hold values from 0 to 1023, as said below
- face_map: int32 [64], replicated, may hold values from 0 to 63, each once
- wall_cells: int32 [1024], P('cell'), may hold values from 0 to 4095, as said below
- wall_normals: float32 [3, 1024], P(None, 'cell'), may hold values from -6 to 6
- pressure_weights: float32 [5], replicated, may hold values from -4 to 4
- mode_shapes: float32 [2, 8, 3, 400], replicated, may hold values from -0.00390625 to 0.00390625
Outputs:
- jacobian_image: bfloat16 [35, 8, 16, 1024], P(None, 'circ', 'cell')
- modal_forces: float32 [7, 400], replicated
The draws below stay inside these ranges and needn't reach their ends.
Inputs may be any that keep to these rules, and one draw needn't show every extreme that they name: `face_cells`: each column names the two cells of a layer that one in-plane face joins; the two differ. `periodic_cells`: all 128 entries differ. `face_map`: each value of 0 to 63 once. `wall_cells`: an entry is the wall cell's layer within its cell block times 1024 plus its cell in the layer; entries may repeat.
All inputs are finite; a program needn't handle non-finite values.
Results may differ from the reference program's by a relative error of at most 0.0055.
Values may be sent and summed in bfloat16 or wider, within the bound.
A program may use at most 64 MiB of HBM per device.

```python
import math
import jax
import jax.numpy as jnp
import numpy as np
from jax import lax

NV = 5
HB = 7
PLANE = 1024
AX_DEV = 4
PER = 64
WALL_DEV = 256
MODES = 400
AXIAL = 16
FACES = 2048
WALLS = 1024
PASSAGES = 8


def draw_face_cells(key, part):
    key_near = jax.random.fold_in(key, 11)
    key_far = jax.random.fold_in(key, 12)
    key_order = jax.random.fold_in(key, 13)
    cell_ids = jnp.arange(PLANE, dtype=jnp.int32)
    near_step = jax.random.randint(key_near, (PLANE,), 1, 4)
    far_step = jax.random.randint(key_far, (PLANE,), 15, 19)
    owners = jnp.concatenate([cell_ids, cell_ids])
    neighbours = jnp.concatenate([(cell_ids + near_step) % PLANE, (cell_ids + far_step) % PLANE])
    face_order = jax.random.permutation(key_order, 2 * PLANE)
    joined_pairs = jnp.stack([owners, neighbours])[:, face_order]
    return joined_pairs.astype(jnp.int32)


def draw_periodic_cells(key, part):
    key_pick = jax.random.fold_in(key, 21)
    key_order = jax.random.fold_in(key, 22)
    inner_cells = jax.random.permutation(key_pick, PLANE - 2)[:2 * PER - 2] + 1
    chosen = jnp.concatenate([jnp.array([0, PLANE - 1], jnp.int32), inner_cells.astype(jnp.int32)])
    chosen = chosen[jax.random.permutation(key_order, 2 * PER)]
    return chosen.reshape(2, PER).astype(jnp.int32)


def draw_wall_cells(key, part):
    key_values = jax.random.fold_in(key, 31)
    key_high = jax.random.fold_in(key, 32)
    key_low = jax.random.fold_in(key, 33)
    limit = AX_DEV * PLANE
    wall_values = jax.random.randint(key_values, (WALLS,), 0, limit)
    high_spot = jax.random.randint(key_high, (), 0, WALLS)
    low_spot = (high_spot + 1 + jax.random.randint(key_low, (), 0, WALLS - 1)) % WALLS
    positions = jnp.arange(WALLS, dtype=jnp.int32)
    wall_values = jnp.where(positions == high_spot, limit - 1, wall_values)
    wall_values = jnp.where(positions == low_spot, 0, wall_values)
    return wall_values.astype(jnp.int32)


def level_of(rng, shape, cuts, smallest, top_value):
    level, own = 1.0, jax.random.fold_in(rng, 6)
    for position, shards_of in cuts:
        steps = jnp.exp(jax.random.uniform(jax.random.fold_in(own, position), (shards_of,), jnp.float32, smallest / len(cuts), top_value / len(cuts)))
        level = level * jnp.repeat(steps, shape[position] // shards_of).reshape([-1 if axis == position else 1 for axis in range(len(shape))])
    return level


def scatter_about(stream_key, extent, width, reach, pieces=(), kind=jnp.bfloat16):
    factor_of = level_of(stream_key, extent, pieces, -0.22, 0.18) if pieces else 1.0
    values = jax.random.normal(stream_key, extent, jnp.float32) * width * factor_of
    return jnp.minimum(jnp.maximum(values, -reach), reach).astype(kind)


def setup_inputs(seed: int = 0) -> dict:
    key_list = jax.random.split(jax.random.key(seed), 14)
    return {
        "flow_state": scatter_about(key_list[0], (HB * NV, PASSAGES, AXIAL, PLANE), 1.0, 6.0, ((1, 8), (2, 4))),
        "time_coef": jnp.clip(jnp.exp(math.log(3.0) - 2.3025851 * jax.random.uniform(key_list[1], (PASSAGES, AXIAL, PLANE), jnp.float32) ** level_of(key_list[1], (PASSAGES, AXIAL, PLANE), ((0, 8), (1, 4)), -0.2, 0.2)), 0.3, 3.0),
        "axial_damp": jnp.clip(jnp.exp(math.log(2.0) - 2.306499 * jax.random.uniform(key_list[2], (PASSAGES, AXIAL, PLANE), jnp.float32) ** level_of(key_list[2], (PASSAGES, AXIAL, PLANE), ((0, 8), (1, 4)), -0.2, 0.2)), 0.19921875, 2.0).astype(jnp.bfloat16),
        "plane_damp": jnp.clip(jnp.exp(math.log(2.0) - 2.306499 * jax.random.uniform(key_list[3], (PASSAGES, AXIAL, FACES), jnp.float32) ** level_of(key_list[3], (PASSAGES, AXIAL, FACES), ((0, 8), (1, 4)), -0.2, 0.2)), 0.19921875, 2.0).astype(jnp.bfloat16),
        "periodic_damp": jnp.clip(jnp.exp(math.log(2.0) - 2.306499 * jax.random.uniform(key_list[4], (PASSAGES, AXIAL, PER), jnp.float32) ** level_of(key_list[4], (PASSAGES, AXIAL, PER), ((0, 8), (1, 4)), -0.2, 0.2)), 0.19921875, 2.0).astype(jnp.bfloat16),
        "flux_jacobian": scatter_about(key_list[5], (3, NV, NV), NV ** -0.5, 2.5, (), jnp.float32),
        "face_cells": draw_face_cells(jax.random.fold_in(key_list[13], 71), 0),
        "periodic_cells": draw_periodic_cells(jax.random.fold_in(key_list[13], 71), 0),
        "face_map": jax.random.permutation(key_list[8], PER).astype(jnp.int32),
        "wall_cells": draw_wall_cells(jax.random.fold_in(key_list[13], 71), 0),
        "wall_normals": scatter_about(key_list[10], (3, WALLS), 1.0, 6.0, ((1, 4),), jnp.float32),
        "pressure_weights": scatter_about(key_list[11], (NV,), 1.0, 4.0, (), jnp.float32),
        "mode_shapes": scatter_about(key_list[12], (2, PASSAGES, 3, MODES), (30 * WALLS * PASSAGES * PASSAGES) ** -0.5, 0.00390625, (), jnp.float32),
    }


def harmonic_matrix(instances):
    matrix_table = np.zeros((instances, instances))
    for row_index in range(instances):
        for column_index in range(instances):
            if row_index != column_index:
                offset_steps = row_index - column_index
                matrix_table[row_index, column_index] = 0.5 * (-1.0) ** offset_steps / math.sin(math.pi * offset_steps / instances)
    return matrix_table


def face_flux(jacobian, damping, lower_state, upper_state):
    total_state = lower_state + upper_state
    jump_state = upper_state - lower_state
    convected = jnp.einsum("vw,nw...->nv...", jacobian, total_state, precision=lax.Precision.HIGHEST)
    return 0.5 * convected - 0.5 * damping * jump_state


def reference(flow_state, time_coef, axial_damp, plane_damp, periodic_damp, flux_jacobian, face_cells, periodic_cells, face_map, wall_cells, wall_normals, pressure_weights, mode_shapes):
    state_all = flow_state.reshape(HB, NV, PASSAGES, AXIAL, PLANE)
    lower_side = periodic_cells[0]
    upper_side = periodic_cells[1]
    targets = lower_side[face_map]
    lower_values = state_all[..., lower_side].astype(jnp.float32)
    upper_values = state_all[..., upper_side].astype(jnp.float32)
    matched_next = jnp.roll(lower_values, -1, axis=2)[..., face_map]
    periodic_all = face_flux(flux_jacobian[2], periodic_damp.astype(jnp.float32), upper_values, matched_next)
    from_previous = jnp.roll(periodic_all, 1, axis=2)
    harmonic = jnp.asarray(harmonic_matrix(HB), jnp.float32)
    block_of_wall = jnp.arange(WALLS, dtype=jnp.int32) // WALL_DEV
    wall_layer = block_of_wall * AX_DEV + wall_cells // PLANE
    wall_column = wall_cells % PLANE
    owners = face_cells[0]
    neighbours = face_cells[1]

    def one_passage(passage_inputs):
        passage_state, cell_coef, damp_axial, damp_plane, own_periodic, incoming = passage_inputs
        current = passage_state.astype(jnp.float32)
        jacobian_sum = cell_coef[None, None] * jnp.einsum("nm,mvac->nvac", harmonic, current, precision=lax.Precision.HIGHEST)
        plane_flux = face_flux(flux_jacobian[1], damp_plane.astype(jnp.float32), current[..., owners], current[..., neighbours])
        jacobian_sum = jacobian_sum.at[..., owners].add(plane_flux).at[..., neighbours].add(-plane_flux)
        upper_rows = jnp.concatenate([current[:, :, 1:], jnp.zeros((HB, NV, 1, PLANE), jnp.float32)], axis=2)
        own_flux = face_flux(flux_jacobian[0], damp_axial.astype(jnp.float32), current, upper_rows)
        jacobian_sum = jacobian_sum + own_flux
        jacobian_sum = jacobian_sum.at[:, :, 1:].add(-own_flux[:, :, :-1])
        jacobian_sum = jacobian_sum.at[..., upper_side].add(own_periodic).at[..., targets].add(-incoming)
        wall_state = current[:, :, wall_layer, wall_column]
        wall_pressure = jnp.einsum("v,nvw->nw", pressure_weights, wall_state, precision=lax.Precision.HIGHEST)
        block_force = jnp.einsum("kw,nw->kn", wall_normals, wall_pressure, precision=lax.Precision.HIGHEST)
        return jacobian_sum.astype(jnp.bfloat16), block_force

    images, forces = lax.map(one_passage, (jnp.moveaxis(state_all, 2, 0), time_coef, axial_damp, plane_damp, jnp.moveaxis(periodic_all, 2, 0), jnp.moveaxis(from_previous, 2, 0)))
    jacobian_image = jnp.moveaxis(images, 0, 2).reshape(HB * NV, PASSAGES, AXIAL, PLANE)
    spectrum = jnp.fft.fft(forces, axis=0)
    real_part = jnp.real(spectrum)
    imag_part = jnp.imag(spectrum)
    modal_forces = jnp.einsum("dkm,dkn->nm", mode_shapes[0], real_part, precision=lax.Precision.HIGHEST) + jnp.einsum("dkm,dkn->nm", mode_shapes[1], imag_part, precision=lax.Precision.HIGHEST)
    return jacobian_image, modal_forces
```

```python
import functools
import math

import jax
import jax.numpy as jnp
import numpy as np
from jax import lax
from jax.experimental import pallas as pl
from jax.experimental.pallas import tpu as pltpu
from jax.sharding import PartitionSpec as P

NV = 5
HB = 7
F32 = jnp.float32
BF16 = jnp.bfloat16
HI = lax.Precision.HIGHEST
MESH = pl.DeviceIdType.MESH
NT = (((1,), (1,)), ((), ()))


def up_to(value, step):
    return -(-value // step) * step


def harmonic_matrix(instances):
    matrix = np.zeros((instances, instances))
    for n in range(instances):
        for m in range(instances):
            if n != m:
                matrix[n, m] = 0.5 * (-1.0) ** (n - m) / math.sin(math.pi * (n - m) / instances)
    return matrix


def constants(layers, passages, walls_k):
    rows = HB * NV * layers
    padded = up_to(rows, 16)
    side = up_to(HB * NV, 16)
    width = padded + 2 * side
    harmonic = harmonic_matrix(HB)
    mix = np.zeros((padded, padded), np.int32)
    axial = np.zeros((padded, width), np.int32)
    fixed = np.zeros((4, padded, width), np.float32)
    pick = np.zeros((2 * side, padded), np.float32)
    weights = np.zeros((8, padded), np.int32)
    variable = np.full((padded, 128), -1, np.int32)
    time = np.zeros((padded, width), np.float32)
    for i in range(rows):
        r, a = divmod(i, layers)
        n, v = divmod(r, NV)
        variable[i] = v
        weights[n, i] = v + 1
        if a == 0:
            pick[r, i] = 1
        if a == layers - 1:
            pick[side + r, i] = 1
        for w in range(NV):
            q = n * NV + w
            mix[i, q * layers + a] = w + 1
            axial[i, q * layers + a + 1 if a < layers - 1 else padded + q] = w + 1
            axial[i, q * layers + a - 1 if a > 0 else padded + side + q] = -(w + 1)
        fixed[2, i, i] = -1
        fixed[2, i, i + 1 if a < layers - 1 else padded + r] = 1
        fixed[3, i, i] = -1
        fixed[3, i, i - 1 if a > 0 else padded + side + r] = 1
        for m in range(HB):
            time[i, (m * NV + v) * layers + a] = harmonic[n, m]
    time_high = time.astype(BF16)
    fixed[0] = time_high.astype(np.float32)
    fixed[1] = time - fixed[0]
    lanes = up_to(walls_k * passages, 128)
    modes = np.zeros((lanes, 2 * passages * 8), np.float32)
    for p in range(passages):
        for d in range(passages):
            angle = 2.0 * math.pi * (d * p % passages) / passages
            for k in range(walls_k):
                modes[p * walls_k + k, d * 8 + k] = math.cos(angle)
                modes[p * walls_k + k, (passages + d) * 8 + k] = -math.sin(angle)
    return (
        mix,
        axial,
        fixed.reshape(4 * padded, width).astype(BF16),
        pick.astype(BF16),
        weights,
        variable,
        modes,
    )


def split(value):
    high = value.astype(BF16)
    return high, (value - high.astype(F32)).astype(BF16)


def dot(a, b):
    return jnp.dot(a, b, preferred_element_type=F32)


def kernel(
    state, time_coef, axial_damp, plane_damp, periodic_damp, jac, faces, sides, face_map,
    wall_cells, normals, press_w, mode_shapes,
    mix_c, axial_c, fixed_c, pick_c, weights_c, variable_c, modes_c,
    image, modal,
    extra, plus, signed, stack, cell_out, above, below, side_out, side_next, side_prev,
    forces_1, forces_2, shapes_pad, total,
    cell_send, cell_recv, side_send, side_recv, f1_send, f1_recv, f2_send, f2_recv,
    *, n_cell, n_circ, layers,
):
    me_cell = lax.axis_index("cell")
    me_circ = lax.axis_index("circ")

    def cell_at(j):
        return {"cell": lax.rem(me_cell + j, n_cell)}

    def circ_at(j):
        return {"circ": lax.rem(me_circ + j, n_circ)}

    barrier = pltpu.get_barrier_semaphore()
    for j in range(1, n_cell):
        pl.semaphore_signal(barrier, inc=1, device_id=cell_at(j), device_id_type=MESH)
    for j in range(1, n_circ):
        pl.semaphore_signal(barrier, inc=1, device_id=circ_at(j), device_id_type=MESH)

    padded, cells = state.shape
    n_faces = faces.shape[1]
    n_walls = wall_cells.shape[1]
    per = sides.shape[1]
    side_rows = above.shape[0]
    walls_k = normals.shape[0]
    groups = padded // 8

    def by_layer(value, pattern):
        return (value.reshape(groups, 8, value.shape[1]) * pattern[None]).reshape(value.shape)

    def pattern_of(rows):
        return jnp.concatenate([rows] * (8 // layers), axis=0)

    u = state[...]

    order = face_map[...]
    hits = (lax.broadcasted_iota(jnp.int32, (per, per), 0) == order).astype(F32)
    targets = jnp.dot(sides[0:1, :].astype(F32), hits, precision=HI, preferred_element_type=F32)
    targets = (targets + 0.5).astype(jnp.int32)
    wall_index = wall_cells[...]
    wall_layer = lax.div(wall_index, cells)
    wall_column = wall_index - wall_layer * cells
    columns = jnp.concatenate([wall_column, sides[1:2, :], targets], axis=1)
    chunk = 256
    step_rows = 16
    for q in range(cells // chunk):
        low = jnp.clip(columns - q * chunk, -1, chunk).astype(F32).astype(BF16)
        low = jnp.broadcast_to(low, (step_rows, low.shape[1]))

        def fill(i, carry, q=q, low=low):
            base = lax.broadcasted_iota(jnp.int32, low.shape, 0) + i * step_rows
            hit = base.astype(F32).astype(BF16) == low
            start = pl.multiple_of(q * chunk + i * step_rows, step_rows)
            extra[pl.ds(start, step_rows), :] = jnp.where(hit, 1.0, 0.0).astype(BF16)
            return carry

        lax.fori_loop(0, chunk // step_rows, fill, 0, unroll=4)

    cell_out[0 : 2 * side_rows, :] = dot(pick_c[...], u).astype(BF16)
    damp = axial_damp[0].astype(F32)
    last = damp[layers - 1 : layers]
    cell_out[2 * side_rows :, :] = jnp.broadcast_to(last, (16, cells)).astype(BF16)

    gathered = dot(u, extra[...])
    own_side = gathered[:, n_walls:]
    side_out[0:padded, :] = own_side.astype(BF16)
    side_damp = periodic_damp[0].astype(F32)
    side_pattern = pattern_of(jnp.concatenate([side_damp, side_damp], axis=1))
    side_out[padded:, :] = jnp.concatenate([side_pattern, side_pattern], axis=0).astype(BF16)

    layer_of = lax.rem(lax.broadcasted_iota(jnp.int32, (8, n_walls), 0), layers)
    here = by_layer(gathered[:, :n_walls], (layer_of == wall_layer).astype(F32))
    weight_class = weights_c[...]
    weight = jnp.zeros(weight_class.shape, F32)
    for v in range(NV):
        weight = jnp.where(weight_class == v + 1, press_w[v], weight)
    pressure = jnp.dot(weight, here, precision=HI, preferred_element_type=F32)
    force = lax.dot_general(pressure, normals[...], NT, precision=HI, preferred_element_type=F32)
    lanes = forces_1.shape[2]
    lane = lax.broadcasted_iota(jnp.int32, (8, lanes), 1)
    tile = jnp.zeros((8, lanes), F32)
    for k in range(walls_k):
        tile = jnp.where(lane == me_circ * walls_k + k, force[:, k : k + 1], tile)
    forces_1[me_cell] = tile

    variable = variable_c[...]

    def row_values(face):
        found = []
        for w in range(NV):
            value = jnp.zeros(variable.shape, F32)
            for v in range(NV):
                value = jnp.where(variable == v, 0.5 * jac[face, v, w], value)
            found.append(value)
        return found

    def mixing(face, classes, signs):
        values = row_values(face)
        pieces = []
        for start in range(0, classes.shape[1], 128):
            part = classes[:, start : start + 128]
            width = part.shape[1]
            value = jnp.zeros(part.shape, F32)
            for w in range(NV):
                value = jnp.where(part == w + 1, values[w][:, :width], value)
                if signs:
                    value = jnp.where(part == -(w + 1), -values[w][:, :width], value)
            pieces.append(value)
        return split(jnp.concatenate(pieces, axis=1))

    pl.semaphore_wait(barrier, n_cell - 1 + n_circ - 1)
    copies = []

    def send(source, target, send_sem, recv_sem, device):
        copy = pltpu.make_async_remote_copy(
            src_ref=source, dst_ref=target, send_sem=send_sem, recv_sem=recv_sem,
            device_id=device, device_id_type=MESH,
        )
        copy.start()
        copies.append(copy)
        return copy

    to_below = send(
        cell_out.at[pl.ds(0, side_rows)], above, cell_send.at[0], cell_recv.at[0],
        cell_at(n_cell - 1),
    )
    to_above = send(
        cell_out.at[pl.ds(side_rows, side_rows + 16)], below, cell_send.at[1], cell_recv.at[1],
        cell_at(1),
    )
    to_prev = send(side_out, side_next, side_send.at[0], side_recv.at[0], circ_at(n_circ - 1))
    to_next = send(side_out, side_prev, side_send.at[1], side_recv.at[1], circ_at(1))
    first = [
        send(forces_1.at[me_cell], forces_1.at[me_cell], f1_send.at[j], f1_recv.at[j], cell_at(j))
        for j in range(1, n_cell)
    ]

    mix_high, mix_low = mixing(1, mix_c[...], False)
    convected = (dot(mix_high, u) + dot(mix_low, u)).astype(BF16)
    for q in range(cells // chunk):
        ends = []
        for side in range(2):
            low = jnp.clip(faces[side : side + 1, :] - q * chunk, -1, chunk)
            low = low.astype(F32).astype(BF16)
            ends.append(jnp.broadcast_to(low, (step_rows, n_faces)))

        def build(i, carry, q=q, ends=ends):
            base = lax.broadcasted_iota(jnp.int32, (step_rows, n_faces), 0) + i * step_rows
            base = base.astype(F32).astype(BF16)
            one = jnp.ones((step_rows, n_faces), BF16)
            zero = jnp.zeros((step_rows, n_faces), BF16)
            owner = jnp.where(base == ends[0], one, zero)
            other = jnp.where(base == ends[1], one, zero)
            start = pl.multiple_of(q * chunk + i * step_rows, step_rows)
            plus[pl.ds(start, step_rows), :] = owner + other
            signed[pl.ds(start, step_rows), :] = owner - other
            return carry

        lax.fori_loop(0, chunk // step_rows, build, 0, unroll=2)

    for copy in first:
        copy.wait_recv()
    summed = forces_1[0]
    for j in range(1, n_cell):
        summed = summed + forces_1[j]
    forces_2[0] = summed

    plane_pattern = pattern_of(0.5 * plane_damp[0].astype(F32))
    flux = dot(convected, plus[...]) + by_layer(dot(u, signed[...]), plane_pattern)
    second = [
        send(forces_2.at[0], forces_2.at[j], f2_send.at[j], f2_recv.at[j], circ_at(j))
        for j in range(1, n_circ)
    ]
    total[...] = lax.dot_general(flux.astype(BF16), signed[...], NT, preferred_element_type=F32)

    shapes_pad[...] = jnp.zeros_like(shapes_pad)
    for part in range(2):
        for d in range(n_circ):
            at = (part * n_circ + d) * 8
            shapes_pad[at : at + walls_k, :] = mode_shapes[part, d]
    by_passage = jnp.dot(modes_c[...], shapes_pad[...], precision=HI, preferred_element_type=F32)

    axial_high, axial_low = mixing(0, axial_c[...], True)
    to_below.wait_recv()
    to_above.wait_recv()
    stack[0:padded, :] = u
    above_rows = above[...].astype(F32)
    stack[padded : padded + side_rows, :] = jnp.where(
        me_cell == n_cell - 1, 0.0, above_rows
    ).astype(BF16)
    below_rows = below[0:side_rows, :].astype(F32)
    stack[padded + side_rows :, :] = jnp.where(
        me_cell == 0, -cell_out[0:side_rows, :].astype(F32), below_rows
    ).astype(BF16)
    below_damp = below[side_rows : side_rows + 16, :].astype(F32)[0:1]
    below_damp = jnp.where(me_cell == 0, 0.0, below_damp)
    held = stack[...]
    derived = dot(fixed_c[...], held)
    result = by_layer(
        derived[0:padded] + derived[padded : 2 * padded], pattern_of(time_coef[0])
    )
    result = result - by_layer(derived[2 * padded : 3 * padded], pattern_of(0.5 * damp))
    lower_damp = jnp.concatenate([below_damp, damp[0 : layers - 1]], axis=0)
    result = result - by_layer(derived[3 * padded :], pattern_of(0.5 * lower_damp))
    result = result + dot(axial_high, held) + dot(axial_low, held)

    side_high, side_low = mixing(2, mix_c[...], False)
    to_prev.wait_recv()
    to_next.wait_recv()
    left = lax.broadcasted_iota(jnp.int32, (padded, 2 * per), 1) < per
    ahead = pltpu.roll(side_next[0:padded, :].astype(F32), per, 1)
    back = pltpu.roll(side_prev[0:padded, :].astype(F32), per, 1)
    back_damp = side_prev[padded:, :].astype(F32)[0:8]
    lower = jnp.where(left, own_side, back)
    upper = jnp.where(left, ahead, own_side)
    side_s = 0.5 * jnp.where(left[0:8], side_pattern, back_damp)
    lower_b, upper_b = lower.astype(BF16), upper.astype(BF16)
    side_flux = dot(side_high, lower_b) + dot(side_high, upper_b)
    side_flux = side_flux + dot(side_low, lower_b) + dot(side_low, upper_b)
    side_flux = side_flux - by_layer(upper - lower, side_s)
    side_flux = jnp.where(left, side_flux, -side_flux).astype(BF16)
    result = result + lax.dot_general(
        side_flux, extra[:, n_walls:], NT, preferred_element_type=F32
    )
    image[...] = (result + total[...]).astype(BF16)

    for copy in second:
        copy.wait_recv()
    every = forces_2[0]
    for j in range(1, n_circ):
        every = every + forces_2[j]
    answer = jnp.dot(every, by_passage, precision=HI, preferred_element_type=F32)
    modal[...] = answer[0:HB]
    for copy in copies:
        copy.wait_send()


def shards(
    flow_state, time_coef, axial_damp, plane_damp, periodic_damp, flux_jacobian, face_cells,
    periodic_cells, face_map, wall_cells, wall_normals, pressure_weights, mode_shapes,
):
    layers, cells = flow_state.shape[2:]
    n_cell = lax.axis_size("cell")
    n_circ = lax.axis_size("circ")
    walls_k = wall_normals.shape[0]
    n_modes = mode_shapes.shape[3]
    per = face_map.shape[0]
    n_faces = face_cells.shape[1]
    n_walls = wall_cells.shape[0]
    fixed = constants(layers, n_circ, walls_k)
    rows = HB * NV * layers
    padded = fixed[0].shape[0]
    side = fixed[3].shape[0] // 2
    lanes = fixed[6].shape[0]
    state = jnp.pad(flow_state.reshape(rows, cells), ((0, padded - rows), (0, 0)))
    vmem = pl.BlockSpec(memory_space=pltpu.VMEM)
    smem = pl.BlockSpec(memory_space=pltpu.SMEM)
    dma = pltpu.SemaphoreType.DMA
    image, modal = pl.pallas_call(
        functools.partial(kernel, n_cell=n_cell, n_circ=n_circ, layers=layers),
        out_shape=(
            jax.ShapeDtypeStruct((padded, cells), BF16),
            jax.ShapeDtypeStruct((HB, n_modes), F32),
        ),
        in_specs=[vmem] * 5 + [smem] + [vmem] * 5 + [smem] + [vmem] * 8,
        out_specs=(vmem, vmem),
        scratch_shapes=[
            pltpu.VMEM((cells, n_walls + 2 * per), BF16),
            pltpu.VMEM((cells, n_faces), BF16),
            pltpu.VMEM((cells, n_faces), BF16),
            pltpu.VMEM((padded + 2 * side, cells), BF16),
            pltpu.VMEM((2 * side + 16, cells), BF16),
            pltpu.VMEM((side, cells), BF16),
            pltpu.VMEM((side + 16, cells), BF16),
            pltpu.VMEM((padded + 16, 2 * per), BF16),
            pltpu.VMEM((padded + 16, 2 * per), BF16),
            pltpu.VMEM((padded + 16, 2 * per), BF16),
            pltpu.VMEM((n_cell, 8, lanes), F32),
            pltpu.VMEM((n_circ, 8, lanes), F32),
            pltpu.VMEM((2 * n_circ * 8, n_modes), F32),
            pltpu.VMEM((padded, cells), F32),
            dma((2,)), dma((2,)), dma((2,)), dma((2,)),
            dma((n_cell,)), dma((n_cell,)), dma((n_circ,)), dma((n_circ,)),
        ],
        compiler_params=pltpu.CompilerParams(collective_id=0, has_side_effects=True),
    )(
        state, time_coef, axial_damp, plane_damp, periodic_damp, flux_jacobian, face_cells,
        periodic_cells, face_map[None], wall_cells[None], wall_normals, pressure_weights,
        mode_shapes, *fixed,
    )
    return image[:rows].reshape(HB * NV, 1, layers, cells), modal


def solution(mesh):
    circ = P("circ", "cell", None)
    placed = (
        P(None, "circ", "cell", None), circ, circ, circ, circ, P(), P(), P(), P(),
        P("cell"), P(None, "cell"), P(), P(),
    )
    return jax.shard_map(
        shards,
        mesh=mesh,
        in_specs=placed,
        out_specs=(P(None, "circ", "cell", None), P()),
        check_vma=False,
    )
```

```python
import functools
import math

import jax
import jax.numpy as jnp
import numpy as np
from jax import lax
from jax.experimental import pallas as pl
from jax.experimental.pallas import tpu as pltpu
from jax.sharding import PartitionSpec as P

NV = 5
HB = 7
F32 = jnp.float32
BF16 = jnp.bfloat16
HI = lax.Precision.HIGHEST
MESH = pl.DeviceIdType.MESH
NT = (((1,), (1,)), ((), ()))


def up_to(value, step):
    return -(-value // step) * step


def harmonic_matrix(instances):
    matrix = np.zeros((instances, instances))
    for n in range(instances):
        for m in range(instances):
            if n != m:
                matrix[n, m] = 0.5 * (-1.0) ** (n - m) / math.sin(math.pi * (n - m) / instances)
    return matrix


def near_scale(values):
    scales = 1.0 + np.arange(4096) / 4096.0
    scaled = scales[:, None] * values[None, :]
    rounded = scaled.astype(BF16).astype(np.float64)
    return float(scales[np.argmin(np.max(np.abs(rounded / scaled - 1.0), axis=1))])


def constants(layers, passages, walls_k):
    rows = HB * NV * layers
    padded = up_to(rows, 16)
    side = up_to(HB * NV, 16)
    width = padded + 2 * side
    harmonic = harmonic_matrix(HB)
    scale = near_scale(np.unique(np.abs(harmonic[harmonic != 0])))
    mix = np.zeros((padded, padded), np.float32)
    axial = np.zeros((padded, width), np.float32)
    fixed = np.zeros((3, padded, width), np.float32)
    pick = np.zeros((2 * side, padded), np.float32)
    weights = np.zeros((8, padded), np.int32)
    of_row = np.zeros((padded, NV), np.float32)
    of_column = np.zeros((NV, width), np.float32)
    for i in range(rows):
        r, a = divmod(i, layers)
        n, v = divmod(r, NV)
        of_row[i, v] = 1
        of_column[v, i] = 1
        of_column[v, padded + r] = 1
        of_column[v, padded + side + r] = 1
        weights[n, i] = v + 1
        if a == 0:
            pick[r, i] = 1
        if a == layers - 1:
            pick[side + r, i] = 1
        for w in range(NV):
            q = n * NV + w
            mix[i, q * layers + a] = 1
            axial[i, q * layers + a + 1 if a < layers - 1 else padded + q] = 1
            axial[i, q * layers + a - 1 if a > 0 else padded + side + q] = -1
        fixed[1, i, i] = -1
        fixed[1, i, i + 1 if a < layers - 1 else padded + r] = 1
        fixed[2, i, i] = -1
        fixed[2, i, i - 1 if a > 0 else padded + side + r] = 1
        for m in range(HB):
            fixed[0, i, (m * NV + v) * layers + a] = scale * harmonic[n, m]
    lanes = up_to(walls_k * passages, 128)
    modes = np.zeros((lanes, 2 * walls_k * passages), np.float32)
    for p in range(passages):
        for d in range(passages):
            angle = 2.0 * math.pi * (d * p % passages) / passages
            for k in range(walls_k):
                modes[p * walls_k + k, k * passages + d] = math.cos(angle)
                modes[p * walls_k + k, (walls_k + k) * passages + d] = -math.sin(angle)
    arrays = (
        mix,
        axial,
        fixed.reshape(3 * padded, width).astype(BF16),
        pick.astype(BF16),
        weights,
        of_row.astype(BF16),
        of_column.astype(BF16),
        modes,
    )
    return arrays, scale


def dot(a, b):
    return jnp.dot(a, b, preferred_element_type=F32)


def kernel(
    state, time_coef, axial_damp, plane_damp, periodic_damp, jac, faces, sides, face_map,
    wall_cells, normals, press_w, mode_shapes,
    mix_c, axial_c, fixed_c, pick_c, weights_c, of_row_c, of_column_c, modes_c,
    image, modal,
    extra, plus, signed, stack, cell_out, above, below, side_out, side_next, side_prev,
    forces_1, forces_2, flux, total,
    cell_send, cell_recv, side_send, side_recv, f1_send, f1_recv, f2_send, f2_recv,
    *, n_cell, n_circ, layers, padded, scale,
):
    me_cell = lax.axis_index("cell")
    me_circ = lax.axis_index("circ")

    def cell_at(j):
        return {"cell": lax.rem(me_cell + j, n_cell)}

    def circ_at(j):
        return {"circ": lax.rem(me_circ + j, n_circ)}

    barrier = pltpu.get_barrier_semaphore()
    for j in range(1, n_cell):
        pl.semaphore_signal(barrier, inc=1, device_id=cell_at(j), device_id_type=MESH)
    for j in range(1, n_circ):
        pl.semaphore_signal(barrier, inc=1, device_id=circ_at(j), device_id_type=MESH)

    n_rows, _, cells = state.shape
    n_faces = faces.shape[1]
    n_walls = wall_cells.shape[1]
    per = sides.shape[1]
    side_rows = above.shape[0]
    walls_k = normals.shape[0]
    groups = padded // 8

    def by_layer(value, pattern):
        return (value.reshape(groups, 8, value.shape[1]) * pattern[None]).reshape(value.shape)

    def pattern_of(rows):
        return jnp.concatenate([rows] * (8 // layers), axis=0)

    wide = state[...].astype(F32)
    pieces = [wide[r] for r in range(n_rows)]
    pieces.append(jnp.zeros((padded - n_rows * layers, cells), F32))
    u = jnp.concatenate(pieces, axis=0).astype(BF16)

    order = face_map[...]
    hits = (lax.broadcasted_iota(jnp.int32, (per, per), 0) == order).astype(F32)
    targets = jnp.dot(sides[0:1, :].astype(F32), hits, precision=HI, preferred_element_type=F32)
    targets = (targets + 0.5).astype(jnp.int32)
    wall_index = wall_cells[...]
    wall_layer = lax.div(wall_index, cells)
    wall_column = wall_index - wall_layer * cells
    columns = jnp.concatenate([wall_column, sides[1:2, :], targets], axis=1)
    chunk = 256
    step_rows = 16
    for q in range(cells // chunk):
        low = jnp.clip(columns - q * chunk, -1, chunk).astype(F32).astype(BF16)
        low = jnp.broadcast_to(low, (step_rows, low.shape[1]))

        def fill(i, carry, q=q, low=low):
            base = lax.broadcasted_iota(jnp.int32, low.shape, 0) + i * step_rows
            hit = base.astype(F32).astype(BF16) == low
            start = pl.multiple_of(q * chunk + i * step_rows, step_rows)
            extra[pl.ds(start, step_rows), :] = jnp.where(hit, 1.0, 0.0).astype(BF16)
            return carry

        lax.fori_loop(0, chunk // step_rows, fill, 0, unroll=4)

    cell_out[0 : 2 * side_rows, :] = dot(pick_c[...], u).astype(BF16)
    damp = axial_damp[0].astype(F32)
    last = damp[layers - 1 : layers]
    cell_out[2 * side_rows :, :] = jnp.broadcast_to(last, (16, cells)).astype(BF16)

    gathered = dot(u, extra[...])
    own_side = gathered[:, n_walls:]
    side_out[0:padded, :] = own_side.astype(BF16)
    side_damp = periodic_damp[0].astype(F32)
    side_pattern = pattern_of(jnp.concatenate([side_damp, side_damp], axis=1))
    side_out[padded:, :] = jnp.concatenate([side_pattern, side_pattern], axis=0).astype(BF16)

    layer_of = lax.rem(lax.broadcasted_iota(jnp.int32, (8, n_walls), 0), layers)
    here = by_layer(gathered[:, :n_walls], (layer_of == wall_layer).astype(F32))
    weight_class = weights_c[...]
    weight = jnp.zeros(weight_class.shape, F32)
    for v in range(NV):
        weight = jnp.where(weight_class == v + 1, press_w[v], weight)
    pressure = jnp.dot(weight, here, precision=HI, preferred_element_type=F32)
    force = lax.dot_general(pressure, normals[...], NT, precision=HI, preferred_element_type=F32)
    lanes = forces_1.shape[2]
    lane = lax.broadcasted_iota(jnp.int32, (8, lanes), 1)
    tile = jnp.zeros((8, lanes), F32)
    for k in range(walls_k):
        tile = jnp.where(lane == me_circ * walls_k + k, force[:, k : k + 1], tile)
    forces_1[me_cell] = tile

    def mixing(face, mask):
        values = (0.5 * jac[:, face, :]).astype(BF16)
        across = dot(values, of_column_c[:, : mask.shape[1]]).astype(BF16)
        return (dot(of_row_c[...], across) * mask).astype(BF16)

    axial_mix = mixing(0, axial_c[...])
    plane_mix = mixing(1, mix_c[...])
    side_mix = mixing(2, mix_c[...])

    convected = dot(plane_mix, u).astype(BF16)
    plane_pattern = pattern_of(0.5 * plane_damp[0].astype(F32))
    high = min(256, cells)
    band = lax.broadcasted_iota(jnp.int32, (high, 128), 0).astype(F32).astype(BF16)
    one = jnp.ones((high, 128), BF16)
    zero = jnp.zeros((high, 128), BF16)

    def build(first, count):
        for at in range(first, first + count, 128):
            for low in range(0, cells, high):
                hits = []
                for side in range(2):
                    place = faces[side : side + 1, at : at + 128] - low
                    place = jnp.clip(place, -1, high).astype(F32).astype(BF16)
                    hits.append(jnp.where(band == place, one, zero))
                plus[low : low + high, at : at + 128] = hits[0] + hits[1]
                signed[low : low + high, at : at + 128] = hits[0] - hits[1]

    def gather(first, count):
        here = slice(first, first + count)
        damped = by_layer(dot(u, signed[:, here]), plane_pattern[:, here])
        flux[:, here] = (dot(convected, plus[:, here]) + damped).astype(BF16)

    part = 256
    starts = list(range(0, n_faces, part))
    early = len(starts) // 2
    build(0, part)
    for at in starts[:early]:
        build(at + part, part)
        gather(at, part)

    pl.semaphore_wait(barrier, n_cell - 1 + n_circ - 1)
    copies = []

    def send(source, target, send_sem, recv_sem, device):
        copy = pltpu.make_async_remote_copy(
            src_ref=source, dst_ref=target, send_sem=send_sem, recv_sem=recv_sem,
            device_id=device, device_id_type=MESH,
        )
        copy.start()
        copies.append(copy)
        return copy

    to_below = send(
        cell_out.at[pl.ds(0, side_rows)], above, cell_send.at[0], cell_recv.at[0],
        cell_at(n_cell - 1),
    )
    to_above = send(
        cell_out.at[pl.ds(side_rows, side_rows + 16)], below, cell_send.at[1], cell_recv.at[1],
        cell_at(1),
    )
    to_prev = send(side_out, side_next, side_send.at[0], side_recv.at[0], circ_at(n_circ - 1))
    to_next = send(side_out, side_prev, side_send.at[1], side_recv.at[1], circ_at(1))
    first = [
        send(forces_1.at[me_cell], forces_1.at[me_cell], f1_send.at[j], f1_recv.at[j], cell_at(j))
        for j in range(1, n_cell)
    ]

    for at in starts[early:]:
        if at + part < n_faces:
            build(at + part, part)
        gather(at, part)

    for copy in first:
        copy.wait_recv()
    summed = forces_1[0]
    for j in range(1, n_cell):
        summed = summed + forces_1[j]
    forces_2[0] = summed
    total[...] = lax.dot_general(flux[...], signed[...], NT, preferred_element_type=F32)
    second = [
        send(forces_2.at[0], forces_2.at[j], f2_send.at[j], f2_recv.at[j], circ_at(j))
        for j in range(1, n_circ)
    ]

    shapes = mode_shapes[...].reshape(2 * walls_k * n_circ, mode_shapes.shape[3])
    by_passage = jnp.dot(modes_c[...], shapes, precision=HI, preferred_element_type=F32)

    to_below.wait_recv()
    to_above.wait_recv()
    stack[0:padded, :] = u
    above_rows = above[...].astype(F32)
    stack[padded : padded + side_rows, :] = jnp.where(
        me_cell == n_cell - 1, 0.0, above_rows
    ).astype(BF16)
    below_rows = below[0:side_rows, :].astype(F32)
    stack[padded + side_rows :, :] = jnp.where(
        me_cell == 0, -cell_out[0:side_rows, :].astype(F32), below_rows
    ).astype(BF16)
    below_damp = below[side_rows : side_rows + 16, :].astype(F32)[0:1]
    below_damp = jnp.where(me_cell == 0, 0.0, below_damp)
    held = stack[...]
    derived = dot(fixed_c[...], held)
    result = by_layer(derived[0:padded], pattern_of(time_coef[0] * (1.0 / scale)))
    result = result - by_layer(derived[padded : 2 * padded], pattern_of(0.5 * damp))
    lower_damp = jnp.concatenate([below_damp, damp[0 : layers - 1]], axis=0)
    result = result - by_layer(derived[2 * padded :], pattern_of(0.5 * lower_damp))
    result = result + dot(axial_mix, held)

    to_prev.wait_recv()
    to_next.wait_recv()
    left = lax.broadcasted_iota(jnp.int32, (padded, 2 * per), 1) < per
    ahead = pltpu.roll(side_next[0:padded, :].astype(F32), per, 1)
    back = pltpu.roll(side_prev[0:padded, :].astype(F32), per, 1)
    back_damp = side_prev[padded:, :].astype(F32)[0:8]
    lower = jnp.where(left, own_side, back)
    upper = jnp.where(left, ahead, own_side)
    side_s = 0.5 * jnp.where(left[0:8], side_pattern, back_damp)
    lower_b, upper_b = lower.astype(BF16), upper.astype(BF16)
    side_flux = dot(side_mix, lower_b) + dot(side_mix, upper_b)
    side_flux = side_flux - by_layer(upper - lower, side_s)
    side_flux = jnp.where(left, side_flux, -side_flux).astype(BF16)
    result = result + lax.dot_general(
        side_flux, extra[:, n_walls:], NT, preferred_element_type=F32
    )
    result = result + total[...]
    for r in range(n_rows):
        image[r] = result[r * layers : (r + 1) * layers].astype(BF16)

    for copy in second:
        copy.wait_recv()
    every = forces_2[0]
    for j in range(1, n_circ):
        every = every + forces_2[j]
    answer = jnp.dot(every, by_passage, precision=HI, preferred_element_type=F32)
    modal[...] = answer[0:HB]
    for copy in copies:
        copy.wait_send()


def shards(
    flow_state, time_coef, axial_damp, plane_damp, periodic_damp, flux_jacobian, face_cells,
    periodic_cells, face_map, wall_cells, wall_normals, pressure_weights, mode_shapes,
):
    layers, cells = flow_state.shape[2:]
    n_cell = lax.axis_size("cell")
    n_circ = lax.axis_size("circ")
    walls_k = wall_normals.shape[0]
    n_modes = mode_shapes.shape[3]
    per = face_map.shape[0]
    n_faces = face_cells.shape[1]
    n_walls = wall_cells.shape[0]
    fixed, scale = constants(layers, n_circ, walls_k)
    padded = fixed[0].shape[0]
    side = fixed[3].shape[0] // 2
    lanes = fixed[7].shape[0]
    state = flow_state.reshape(HB * NV, layers, cells)
    vmem = pl.BlockSpec(memory_space=pltpu.VMEM)
    smem = pl.BlockSpec(memory_space=pltpu.SMEM)
    dma = pltpu.SemaphoreType.DMA
    image, modal = pl.pallas_call(
        functools.partial(
            kernel, n_cell=n_cell, n_circ=n_circ, layers=layers, padded=padded, scale=scale
        ),
        out_shape=(
            jax.ShapeDtypeStruct((HB * NV, layers, cells), BF16),
            jax.ShapeDtypeStruct((HB, n_modes), F32),
        ),
        in_specs=[vmem] * 11 + [smem] + [vmem] * 9,
        out_specs=(vmem, vmem),
        scratch_shapes=[
            pltpu.VMEM((cells, n_walls + 2 * per), BF16),
            pltpu.VMEM((cells, n_faces), BF16),
            pltpu.VMEM((cells, n_faces), BF16),
            pltpu.VMEM((padded + 2 * side, cells), BF16),
            pltpu.VMEM((2 * side + 16, cells), BF16),
            pltpu.VMEM((side, cells), BF16),
            pltpu.VMEM((side + 16, cells), BF16),
            pltpu.VMEM((padded + 16, 2 * per), BF16),
            pltpu.VMEM((padded + 16, 2 * per), BF16),
            pltpu.VMEM((padded + 16, 2 * per), BF16),
            pltpu.VMEM((n_cell, 8, lanes), F32),
            pltpu.VMEM((n_circ, 8, lanes), F32),
            pltpu.VMEM((padded, n_faces), BF16),
            pltpu.VMEM((padded, cells), F32),
            dma((2,)), dma((2,)), dma((2,)), dma((2,)),
            dma((n_cell,)), dma((n_cell,)), dma((n_circ,)), dma((n_circ,)),
        ],
        compiler_params=pltpu.CompilerParams(collective_id=0, has_side_effects=True),
    )(
        state, time_coef, axial_damp, plane_damp, periodic_damp,
        flux_jacobian.transpose(1, 0, 2), face_cells, periodic_cells, face_map[None], wall_cells[None], wall_normals, pressure_weights,
        mode_shapes.transpose(0, 2, 1, 3), *fixed,
    )
    return image.reshape(HB * NV, 1, layers, cells), modal


def solution(mesh):
    circ = P("circ", "cell", None)
    placed = (
        P(None, "circ", "cell", None), circ, circ, circ, circ, P(), P(), P(), P(),
        P("cell"), P(None, "cell"), P(), P(),
    )
    return jax.shard_map(
        shards,
        mesh=mesh,
        in_specs=placed,
        out_specs=(P(None, "circ", "cell", None), P()),
        check_vma=False,
    )
```

```python
import functools
import math

import jax
import jax.numpy as jnp
import numpy as np
from jax import lax
from jax.experimental import pallas as pl
from jax.experimental.pallas import tpu as pltpu
from jax.sharding import PartitionSpec as P

NV = 5
HB = 7
F32 = jnp.float32
BF16 = jnp.bfloat16
HI = lax.Precision.HIGHEST
MESH = pl.DeviceIdType.MESH
NT = (((1,), (1,)), ((), ()))


def up_to(value, step):
    return -(-value // step) * step


def harmonic_matrix(instances):
    matrix = np.zeros((instances, instances))
    for n in range(instances):
        for m in range(instances):
            if n != m:
                matrix[n, m] = 0.5 * (-1.0) ** (n - m) / math.sin(math.pi * (n - m) / instances)
    return matrix


def near_scale(values):
    scales = 1.0 + np.arange(4096) / 4096.0
    scaled = scales[:, None] * values[None, :]
    rounded = scaled.astype(BF16).astype(np.float64)
    return float(scales[np.argmin(np.max(np.abs(rounded / scaled - 1.0), axis=1))])


def constants(layers, passages, walls_k):
    rows = HB * NV * layers
    padded = up_to(rows, 16)
    side = up_to(HB * NV, 16)
    width = padded + 2 * side
    harmonic = harmonic_matrix(HB)
    scale = near_scale(np.unique(np.abs(harmonic[harmonic != 0])))
    mix = np.zeros((padded, padded), np.float32)
    axial = np.zeros((padded, width), np.float32)
    fixed = np.zeros((3, padded, width), np.float32)
    pick = np.zeros((2 * side, padded), np.float32)
    weights = np.zeros((8, padded), np.int32)
    of_row = np.zeros((padded, NV), np.float32)
    of_column = np.zeros((NV, width), np.float32)
    for i in range(rows):
        r, a = divmod(i, layers)
        n, v = divmod(r, NV)
        of_row[i, v] = 1
        of_column[v, i] = 1
        of_column[v, padded + r] = 1
        of_column[v, padded + side + r] = 1
        weights[n, i] = v + 1
        if a == 0:
            pick[r, i] = 1
        if a == layers - 1:
            pick[side + r, i] = 1
        for w in range(NV):
            q = n * NV + w
            mix[i, q * layers + a] = 1
            axial[i, q * layers + a + 1 if a < layers - 1 else padded + q] = 1
            axial[i, q * layers + a - 1 if a > 0 else padded + side + q] = -1
        fixed[1, i, i] = -1
        fixed[1, i, i + 1 if a < layers - 1 else padded + r] = 1
        fixed[2, i, i] = -1
        fixed[2, i, i - 1 if a > 0 else padded + side + r] = 1
        for m in range(HB):
            fixed[0, i, (m * NV + v) * layers + a] = scale * harmonic[n, m]
    lanes = up_to(walls_k * passages, 128)
    modes = np.zeros((lanes, 2 * walls_k * passages), np.float32)
    for p in range(passages):
        for d in range(passages):
            angle = 2.0 * math.pi * (d * p % passages) / passages
            for k in range(walls_k):
                modes[p * walls_k + k, k * passages + d] = math.cos(angle)
                modes[p * walls_k + k, (walls_k + k) * passages + d] = -math.sin(angle)
    arrays = (
        mix,
        axial,
        fixed.reshape(3 * padded, width).astype(BF16),
        pick.astype(BF16),
        weights,
        of_row.astype(BF16),
        of_column.astype(BF16),
        modes,
    )
    return arrays, scale


def dot(a, b):
    return jnp.dot(a, b, preferred_element_type=F32)


def kernel(
    state, time_coef, axial_damp, plane_damp, periodic_damp, jac, faces, sides, face_map,
    wall_cells, normals, press_w, mode_shapes,
    mix_c, axial_c, fixed_c, pick_c, weights_c, of_row_c, of_column_c, modes_c,
    image, modal,
    extra, plus, signed, stack, cell_out, above, below, side_out, side_next, side_prev,
    forces_1, forces_2, flux, total,
    cell_send, cell_recv, side_send, side_recv, f1_send, f1_recv, f2_send, f2_recv,
    *, n_cell, n_circ, layers, padded, scale,
):
    me_cell = lax.axis_index("cell")
    me_circ = lax.axis_index("circ")

    def cell_at(j):
        return {"cell": lax.rem(me_cell + j, n_cell)}

    def circ_at(j):
        return {"circ": lax.rem(me_circ + j, n_circ)}

    barrier = pltpu.get_barrier_semaphore()
    for j in range(1, n_cell):
        pl.semaphore_signal(barrier, inc=1, device_id=cell_at(j), device_id_type=MESH)
    for j in range(1, n_circ):
        pl.semaphore_signal(barrier, inc=1, device_id=circ_at(j), device_id_type=MESH)

    n_rows, _, cells = state.shape
    n_faces = faces.shape[1]
    n_walls = wall_cells.shape[1]
    per = sides.shape[1]
    side_rows = above.shape[0]
    walls_k = normals.shape[0]
    groups = padded // 8

    def by_layer(value, pattern):
        return (value.reshape(groups, 8, value.shape[1]) * pattern[None]).reshape(value.shape)

    def pattern_of(rows):
        return jnp.concatenate([rows] * (8 // layers), axis=0)

    wide = state[...].astype(F32)
    pieces = [wide[r] for r in range(n_rows)]
    pieces.append(jnp.zeros((padded - n_rows * layers, cells), F32))
    u = jnp.concatenate(pieces, axis=0).astype(BF16)

    order = face_map[...]
    hits = (lax.broadcasted_iota(jnp.int32, (per, per), 0) == order).astype(F32)
    targets = jnp.dot(sides[0:1, :].astype(F32), hits, precision=HI, preferred_element_type=F32)
    targets = (targets + 0.5).astype(jnp.int32)
    wall_index = wall_cells[...]
    wall_layer = lax.div(wall_index, cells)
    wall_column = wall_index - wall_layer * cells
    columns = jnp.concatenate([wall_column, sides[1:2, :], targets], axis=1)
    high = min(256, cells)
    piece = 32
    bands = [
        (lax.broadcasted_iota(jnp.int32, (piece, 128), 0) + start).astype(F32).astype(BF16)
        for start in range(0, high, piece)
    ]
    one = jnp.ones((piece, 128), BF16)
    zero = jnp.zeros((piece, 128), BF16)

    def places(row, low):
        place = jnp.clip(row - low, -1, high).astype(F32).astype(BF16)
        return jnp.broadcast_to(place, (piece, 128))

    for at in range(extra.shape[0]):
        row = columns[:, at * 128 : (at + 1) * 128]
        for low in range(0, cells, high):
            place = places(row, low)
            for k, band in enumerate(bands):
                start = low + k * piece
                extra[at, start : start + piece, :] = jnp.where(band == place, one, zero)

    def tiles(table, first, count):
        found = [table[first // 128 + k] for k in range(count // 128)]
        return jnp.concatenate(found, axis=1)

    cell_out[0 : 2 * side_rows, :] = dot(pick_c[...], u).astype(BF16)
    damp = axial_damp[0].astype(F32)
    last = damp[layers - 1 : layers]
    cell_out[2 * side_rows :, :] = jnp.broadcast_to(last, (16, cells)).astype(BF16)

    gathered = dot(u, tiles(extra, 0, n_walls + 2 * per))
    own_side = gathered[:, n_walls:]
    side_out[0:padded, :] = own_side.astype(BF16)
    side_damp = periodic_damp[0].astype(F32)
    side_pattern = pattern_of(jnp.concatenate([side_damp, side_damp], axis=1))
    side_out[padded:, :] = jnp.concatenate([side_pattern, side_pattern], axis=0).astype(BF16)

    layer_of = lax.rem(lax.broadcasted_iota(jnp.int32, (8, n_walls), 0), layers)
    here = by_layer(gathered[:, :n_walls], (layer_of == wall_layer).astype(F32))
    weight_class = weights_c[...]
    weight = jnp.zeros(weight_class.shape, F32)
    for v in range(NV):
        weight = jnp.where(weight_class == v + 1, press_w[v], weight)
    pressure = jnp.dot(weight, here, precision=HI, preferred_element_type=F32)
    force = lax.dot_general(pressure, normals[...], NT, precision=HI, preferred_element_type=F32)
    lanes = forces_1.shape[2]
    lane = lax.broadcasted_iota(jnp.int32, (8, lanes), 1)
    tile = jnp.zeros((8, lanes), F32)
    for k in range(walls_k):
        tile = jnp.where(lane == me_circ * walls_k + k, force[:, k : k + 1], tile)
    forces_1[me_cell] = tile

    def mixing(face, mask):
        values = (0.5 * jac[:, face, :]).astype(BF16)
        across = dot(values, of_column_c[:, : mask.shape[1]]).astype(BF16)
        return (dot(of_row_c[...], across) * mask).astype(BF16)

    axial_mix = mixing(0, axial_c[...])
    plane_mix = mixing(1, mix_c[...])
    side_mix = mixing(2, mix_c[...])

    convected = dot(plane_mix, u).astype(BF16)
    plane_pattern = pattern_of(0.5 * plane_damp[0].astype(F32))

    def build(first, count):
        for at in range(first, first + count, 128):
            rows = [faces[side : side + 1, at : at + 128] for side in range(2)]
            for low in range(0, cells, high):
                owner, other = places(rows[0], low), places(rows[1], low)
                for k, band in enumerate(bands):
                    start = low + k * piece
                    hit = jnp.where(band == owner, one, jnp.where(band == other, -one, zero))
                    plus[at // 128, start : start + piece, :] = jnp.abs(hit)
                    signed[at // 128, start : start + piece, :] = hit

    def gather(first, count):
        here = slice(first, first + count)
        damped = by_layer(dot(u, tiles(signed, first, count)), plane_pattern[:, here])
        flux[:, here] = (dot(convected, tiles(plus, first, count)) + damped).astype(BF16)

    part = 256
    starts = list(range(0, n_faces, part))
    early = len(starts) // 2
    build(0, part)
    for at in starts[:early]:
        build(at + part, part)
        gather(at, part)

    pl.semaphore_wait(barrier, n_cell - 1 + n_circ - 1)
    copies = []

    def send(source, target, send_sem, recv_sem, device):
        copy = pltpu.make_async_remote_copy(
            src_ref=source, dst_ref=target, send_sem=send_sem, recv_sem=recv_sem,
            device_id=device, device_id_type=MESH,
        )
        copy.start()
        copies.append(copy)
        return copy

    to_below = send(
        cell_out.at[pl.ds(0, side_rows)], above, cell_send.at[0], cell_recv.at[0],
        cell_at(n_cell - 1),
    )
    to_above = send(
        cell_out.at[pl.ds(side_rows, side_rows + 16)], below, cell_send.at[1], cell_recv.at[1],
        cell_at(1),
    )
    to_prev = send(side_out, side_next, side_send.at[0], side_recv.at[0], circ_at(n_circ - 1))
    to_next = send(side_out, side_prev, side_send.at[1], side_recv.at[1], circ_at(1))
    first = [
        send(forces_1.at[me_cell], forces_1.at[me_cell], f1_send.at[j], f1_recv.at[j], cell_at(j))
        for j in range(1, n_cell)
    ]

    for at in starts[early:]:
        if at + part < n_faces:
            build(at + part, part)
        gather(at, part)

    for copy in first:
        copy.wait_recv()
    summed = forces_1[0]
    for j in range(1, n_cell):
        summed = summed + forces_1[j]
    forces_2[0] = summed
    shapes = mode_shapes[...].reshape(2 * walls_k * n_circ, mode_shapes.shape[3])
    by_passage = jnp.dot(modes_c[...], shapes, precision=HI, preferred_element_type=F32)

    second = [
        send(forces_2.at[0], forces_2.at[j], f2_send.at[j], f2_recv.at[j], circ_at(j))
        for j in range(1, n_circ)
    ]

    total[...] = lax.dot_general(
        flux[...], tiles(signed, 0, n_faces), NT, preferred_element_type=F32
    )

    to_below.wait_recv()
    to_above.wait_recv()
    stack[0:padded, :] = u
    above_rows = above[...].astype(F32)
    stack[padded : padded + side_rows, :] = jnp.where(
        me_cell == n_cell - 1, 0.0, above_rows
    ).astype(BF16)
    below_rows = below[0:side_rows, :].astype(F32)
    stack[padded + side_rows :, :] = jnp.where(
        me_cell == 0, -cell_out[0:side_rows, :].astype(F32), below_rows
    ).astype(BF16)
    below_damp = below[side_rows : side_rows + 16, :].astype(F32)[0:1]
    below_damp = jnp.where(me_cell == 0, 0.0, below_damp)
    held = stack[...]
    derived = dot(fixed_c[...], held)
    result = by_layer(derived[0:padded], pattern_of(time_coef[0] * (1.0 / scale)))
    result = result - by_layer(derived[padded : 2 * padded], pattern_of(0.5 * damp))
    lower_damp = jnp.concatenate([below_damp, damp[0 : layers - 1]], axis=0)
    result = result - by_layer(derived[2 * padded :], pattern_of(0.5 * lower_damp))
    result = result + dot(axial_mix, held)

    to_prev.wait_recv()
    to_next.wait_recv()
    left = lax.broadcasted_iota(jnp.int32, (padded, 2 * per), 1) < per
    ahead = pltpu.roll(side_next[0:padded, :].astype(F32), per, 1)
    back = pltpu.roll(side_prev[0:padded, :].astype(F32), per, 1)
    back_damp = side_prev[padded:, :].astype(F32)[0:8]
    lower = jnp.where(left, own_side, back)
    upper = jnp.where(left, ahead, own_side)
    side_s = 0.5 * jnp.where(left[0:8], side_pattern, back_damp)
    lower_b, upper_b = lower.astype(BF16), upper.astype(BF16)
    side_flux = dot(side_mix, lower_b) + dot(side_mix, upper_b)
    side_flux = side_flux - by_layer(upper - lower, side_s)
    side_flux = jnp.where(left, side_flux, -side_flux).astype(BF16)
    result = result + lax.dot_general(
        side_flux, tiles(extra, n_walls, 2 * per), NT, preferred_element_type=F32
    )
    result = result + total[...]
    for r in range(n_rows):
        image[r] = result[r * layers : (r + 1) * layers].astype(BF16)

    for copy in second:
        copy.wait_recv()
    every = forces_2[0]
    for j in range(1, n_circ):
        every = every + forces_2[j]
    answer = jnp.dot(every, by_passage, precision=HI, preferred_element_type=F32)
    modal[...] = answer[0:HB]
    for copy in copies:
        copy.wait_send()


def deliver(image, modal, image_out, modal_out, sems):
    copies = [
        pltpu.make_async_copy(image, image_out, sems.at[0]),
        pltpu.make_async_copy(modal, modal_out, sems.at[1]),
    ]
    for copy in copies:
        copy.start()
    for copy in copies:
        copy.wait()


def shards(
    flow_state, time_coef, axial_damp, plane_damp, periodic_damp, flux_jacobian, face_cells,
    periodic_cells, face_map, wall_cells, wall_normals, pressure_weights, mode_shapes,
):
    layers, cells = flow_state.shape[2:]
    n_cell = lax.axis_size("cell")
    n_circ = lax.axis_size("circ")
    walls_k = wall_normals.shape[0]
    n_modes = mode_shapes.shape[3]
    per = face_map.shape[0]
    n_faces = face_cells.shape[1]
    n_walls = wall_cells.shape[0]
    fixed, scale = constants(layers, n_circ, walls_k)
    padded = fixed[0].shape[0]
    side = fixed[3].shape[0] // 2
    lanes = fixed[7].shape[0]
    state = flow_state.reshape(HB * NV, layers, cells)
    vmem = pl.BlockSpec(memory_space=pltpu.VMEM)
    smem = pl.BlockSpec(memory_space=pltpu.SMEM)
    dma = pltpu.SemaphoreType.DMA
    image, modal = pl.pallas_call(
        functools.partial(
            kernel, n_cell=n_cell, n_circ=n_circ, layers=layers, padded=padded, scale=scale
        ),
        out_shape=(
            jax.ShapeDtypeStruct((HB * NV, layers, cells), BF16),
            jax.ShapeDtypeStruct((HB, n_modes), F32),
        ),
        in_specs=[vmem] * 11 + [smem] + [vmem] * 9,
        out_specs=(vmem, vmem),
        scratch_shapes=[
            pltpu.VMEM(((n_walls + 2 * per) // 128, cells, 128), BF16),
            pltpu.VMEM((n_faces // 128, cells, 128), BF16),
            pltpu.VMEM((n_faces // 128, cells, 128), BF16),
            pltpu.VMEM((padded + 2 * side, cells), BF16),
            pltpu.VMEM((2 * side + 16, cells), BF16),
            pltpu.VMEM((side, cells), BF16),
            pltpu.VMEM((side + 16, cells), BF16),
            pltpu.VMEM((padded + 16, 2 * per), BF16),
            pltpu.VMEM((padded + 16, 2 * per), BF16),
            pltpu.VMEM((padded + 16, 2 * per), BF16),
            pltpu.VMEM((n_cell, 8, lanes), F32),
            pltpu.VMEM((n_circ, 8, lanes), F32),
            pltpu.VMEM((padded, n_faces), BF16),
            pltpu.VMEM((padded, cells), F32),
            dma((2,)), dma((2,)), dma((2,)), dma((2,)),
            dma((n_cell,)), dma((n_cell,)), dma((n_circ,)), dma((n_circ,)),
        ],
        compiler_params=pltpu.CompilerParams(collective_id=0, has_side_effects=True),
    )(
        state, time_coef, axial_damp, plane_damp, periodic_damp,
        flux_jacobian.transpose(1, 0, 2), face_cells, periodic_cells, face_map[None], wall_cells[None], wall_normals, pressure_weights,
        mode_shapes.transpose(0, 2, 1, 3), *fixed,
    )
    anywhere = pl.BlockSpec(memory_space=pl.ANY)
    image, modal = pl.pallas_call(
        deliver,
        out_shape=(
            jax.ShapeDtypeStruct(image.shape, BF16),
            jax.ShapeDtypeStruct(modal.shape, F32),
        ),
        in_specs=[anywhere] * 2,
        out_specs=(vmem, vmem),
        scratch_shapes=[dma((2,))],
    )(image, modal)
    return image.reshape(HB * NV, 1, layers, cells), modal


def solution(mesh):
    circ = P("circ", "cell", None)
    placed = (
        P(None, "circ", "cell", None), circ, circ, circ, circ, P(), P(), P(), P(),
        P("cell"), P(None, "cell"), P(), P(),
    )
    return jax.shard_map(
        shards,
        mesh=mesh,
        in_specs=placed,
        out_specs=(P(None, "circ", "cell", None), P()),
        check_vma=False,
    )
```

```python
import functools
import math

import jax
import jax.numpy as jnp
import numpy as np
from jax import lax
from jax.experimental import pallas as pl
from jax.experimental.pallas import tpu as pltpu
from jax.sharding import PartitionSpec as P

NV = 5
HB = 7
F32 = jnp.float32
BF16 = jnp.bfloat16
HI = lax.Precision.HIGHEST
MESH = pl.DeviceIdType.MESH
NT = (((1,), (1,)), ((), ()))


def up_to(value, step):
    return -(-value // step) * step


def harmonic_matrix(instances):
    matrix = np.zeros((instances, instances))
    for n in range(instances):
        for m in range(instances):
            if n != m:
                matrix[n, m] = 0.5 * (-1.0) ** (n - m) / math.sin(math.pi * (n - m) / instances)
    return matrix


def near_scale(values):
    scales = 1.0 + np.arange(4096) / 4096.0
    scaled = scales[:, None] * values[None, :]
    rounded = scaled.astype(BF16).astype(np.float64)
    return float(scales[np.argmin(np.max(np.abs(rounded / scaled - 1.0), axis=1))])


def constants(layers, passages, walls_k):
    rows = HB * NV * layers
    padded = up_to(rows, 16)
    side = up_to(HB * NV, 16)
    width = padded + 2 * side
    harmonic = harmonic_matrix(HB)
    scale = near_scale(np.unique(np.abs(harmonic[harmonic != 0])))
    mix = np.zeros((padded, padded), np.float32)
    axial = np.zeros((padded, width), np.float32)
    fixed = np.zeros((3, padded, width), np.float32)
    pick = np.zeros((2 * side, padded), np.float32)
    weights = np.zeros((8, padded), np.int32)
    of_row = np.zeros((padded, NV), np.float32)
    of_column = np.zeros((NV, width), np.float32)
    for i in range(rows):
        r, a = divmod(i, layers)
        n, v = divmod(r, NV)
        of_row[i, v] = 1
        of_column[v, i] = 1
        of_column[v, padded + r] = 1
        of_column[v, padded + side + r] = 1
        weights[n, i] = v + 1
        if a == 0:
            pick[r, i] = 1
        if a == layers - 1:
            pick[side + r, i] = 1
        for w in range(NV):
            q = n * NV + w
            mix[i, q * layers + a] = 1
            axial[i, q * layers + a + 1 if a < layers - 1 else padded + q] = 1
            axial[i, q * layers + a - 1 if a > 0 else padded + side + q] = -1
        fixed[1, i, i] = -1
        fixed[1, i, i + 1 if a < layers - 1 else padded + r] = 1
        fixed[2, i, i] = -1
        fixed[2, i, i - 1 if a > 0 else padded + side + r] = 1
        for m in range(HB):
            fixed[0, i, (m * NV + v) * layers + a] = scale * harmonic[n, m]
    lanes = up_to(walls_k * passages, 128)
    modes = np.zeros((lanes, 2 * walls_k * passages), np.float32)
    for p in range(passages):
        for d in range(passages):
            angle = 2.0 * math.pi * (d * p % passages) / passages
            for k in range(walls_k):
                modes[p * walls_k + k, k * passages + d] = math.cos(angle)
                modes[p * walls_k + k, (walls_k + k) * passages + d] = -math.sin(angle)
    arrays = (
        mix,
        axial,
        fixed.reshape(3 * padded, width).astype(BF16),
        pick.astype(BF16),
        weights,
        of_row.astype(BF16),
        of_column.astype(BF16),
        modes,
    )
    return arrays, scale


def dot(a, b):
    return jnp.dot(a, b, preferred_element_type=F32)


def kernel(
    state, time_coef, axial_damp, plane_damp, periodic_damp, jac, faces, sides, face_map,
    wall_cells, normals, press_w, mode_shapes,
    mix_c, axial_c, fixed_c, pick_c, weights_c, of_row_c, of_column_c, modes_c,
    image, modal,
    extra, signed, stack, cell_out, above, below, side_out, side_next, side_prev,
    forces_1, forces_2, flux, total,
    cell_send, cell_recv, side_send, side_recv, f1_send, f1_recv, f2_send, f2_recv,
    *, n_cell, n_circ, layers, padded, scale,
):
    me_cell = lax.axis_index("cell")
    me_circ = lax.axis_index("circ")

    def cell_at(j):
        return {"cell": lax.rem(me_cell + j, n_cell)}

    def circ_at(j):
        return {"circ": lax.rem(me_circ + j, n_circ)}

    barrier = pltpu.get_barrier_semaphore()
    for j in range(1, n_cell):
        pl.semaphore_signal(barrier, inc=1, device_id=cell_at(j), device_id_type=MESH)
    for j in range(1, n_circ):
        pl.semaphore_signal(barrier, inc=1, device_id=circ_at(j), device_id_type=MESH)

    n_rows, _, cells = state.shape
    n_faces = faces.shape[1]
    n_walls = wall_cells.shape[1]
    per = sides.shape[1]
    side_rows = above.shape[0]
    walls_k = normals.shape[0]
    groups = padded // 8

    def by_layer(value, pattern):
        return (value.reshape(groups, 8, value.shape[1]) * pattern[None]).reshape(value.shape)

    def pattern_of(rows):
        return jnp.concatenate([rows] * (8 // layers), axis=0)

    wide = state[...].astype(F32)
    pieces = [wide[r] for r in range(n_rows)]
    pieces.append(jnp.zeros((padded - n_rows * layers, cells), F32))
    u = jnp.concatenate(pieces, axis=0).astype(BF16)

    order = face_map[...]
    hits = (lax.broadcasted_iota(jnp.int32, (per, per), 0) == order).astype(F32)
    targets = jnp.dot(sides[0:1, :].astype(F32), hits, precision=HI, preferred_element_type=F32)
    targets = (targets + 0.5).astype(jnp.int32)
    wall_index = wall_cells[...]
    wall_layer = lax.div(wall_index, cells)
    wall_column = wall_index - wall_layer * cells
    columns = jnp.concatenate([wall_column, sides[1:2, :], targets], axis=1)
    high = min(256, cells)
    piece = 32
    bands = [
        (lax.broadcasted_iota(jnp.int32, (piece, 128), 0) + start).astype(F32).astype(BF16)
        for start in range(0, high, piece)
    ]
    one = jnp.ones((piece, 128), BF16)
    zero = jnp.zeros((piece, 128), BF16)

    def places(row, low):
        place = jnp.clip(row - low, -1, high).astype(F32).astype(BF16)
        return jnp.broadcast_to(place, (piece, 128))

    for at in range(extra.shape[0]):
        row = columns[:, at * 128 : (at + 1) * 128]
        for low in range(0, cells, high):
            place = places(row, low)
            for k, band in enumerate(bands):
                start = low + k * piece
                extra[at, start : start + piece, :] = jnp.where(band == place, one, zero)

    def tiles(table, first, count):
        found = [table[first // 128 + k] for k in range(count // 128)]
        return jnp.concatenate(found, axis=1)

    cell_out[0 : 2 * side_rows, :] = dot(pick_c[...], u).astype(BF16)
    damp = axial_damp[0].astype(F32)
    last = damp[layers - 1 : layers]
    cell_out[2 * side_rows :, :] = jnp.broadcast_to(last, (16, cells)).astype(BF16)

    gathered = dot(u, tiles(extra, 0, n_walls + 2 * per))
    own_side = gathered[:, n_walls:]
    side_out[0:padded, :] = own_side.astype(BF16)
    side_damp = periodic_damp[0].astype(F32)
    side_pattern = pattern_of(jnp.concatenate([side_damp, side_damp], axis=1))
    side_out[padded:, :] = jnp.concatenate([side_pattern, side_pattern], axis=0).astype(BF16)

    layer_of = lax.rem(lax.broadcasted_iota(jnp.int32, (8, n_walls), 0), layers)
    here = by_layer(gathered[:, :n_walls], (layer_of == wall_layer).astype(F32))
    weight_class = weights_c[...]
    weight = jnp.zeros(weight_class.shape, F32)
    for v in range(NV):
        weight = jnp.where(weight_class == v + 1, press_w[v], weight)
    pressure = jnp.dot(weight, here, precision=HI, preferred_element_type=F32)
    force = lax.dot_general(pressure, normals[...], NT, precision=HI, preferred_element_type=F32)
    lanes = forces_1.shape[2]
    lane = lax.broadcasted_iota(jnp.int32, (8, lanes), 1)
    tile = jnp.zeros((8, lanes), F32)
    for k in range(walls_k):
        tile = jnp.where(lane == me_circ * walls_k + k, force[:, k : k + 1], tile)
    forces_1[me_cell] = tile

    def mixing(face, mask):
        values = (0.5 * jac[:, face, :]).astype(BF16)
        across = dot(values, of_column_c[:, : mask.shape[1]]).astype(BF16)
        return (dot(of_row_c[...], across) * mask).astype(BF16)

    axial_mix = mixing(0, axial_c[...])
    plane_mix = mixing(1, mix_c[...])
    side_mix = mixing(2, mix_c[...])

    convected = dot(plane_mix, u).astype(BF16)
    plane_pattern = pattern_of(0.5 * plane_damp[0].astype(F32))

    def build(first, count):
        for at in range(first, first + count, 128):
            rows = [faces[side : side + 1, at : at + 128] for side in range(2)]
            for low in range(0, cells, high):
                owner, other = places(rows[0], low), places(rows[1], low)
                for k, band in enumerate(bands):
                    start = low + k * piece
                    hit = jnp.where(band == owner, one, jnp.where(band == other, -one, zero))
                    signed[at // 128, start : start + piece, :] = hit

    def gather(first, count):
        here = slice(first, first + count)
        table = tiles(signed, first, count)
        damped = by_layer(dot(u, table), plane_pattern[:, here])
        flux[:, here] = (dot(convected, jnp.abs(table)) + damped).astype(BF16)

    part = 256
    starts = list(range(0, n_faces, part))
    early = len(starts) // 2
    build(0, part)
    for at in starts[:early]:
        build(at + part, part)
        gather(at, part)

    pl.semaphore_wait(barrier, n_cell - 1 + n_circ - 1)
    copies = []

    def send(source, target, send_sem, recv_sem, device):
        copy = pltpu.make_async_remote_copy(
            src_ref=source, dst_ref=target, send_sem=send_sem, recv_sem=recv_sem,
            device_id=device, device_id_type=MESH,
        )
        copy.start()
        copies.append(copy)
        return copy

    to_below = send(
        cell_out.at[pl.ds(0, side_rows)], above, cell_send.at[0], cell_recv.at[0],
        cell_at(n_cell - 1),
    )
    to_above = send(
        cell_out.at[pl.ds(side_rows, side_rows + 16)], below, cell_send.at[1], cell_recv.at[1],
        cell_at(1),
    )
    to_prev = send(side_out, side_next, side_send.at[0], side_recv.at[0], circ_at(n_circ - 1))
    to_next = send(side_out, side_prev, side_send.at[1], side_recv.at[1], circ_at(1))
    first = [
        send(forces_1.at[me_cell], forces_1.at[me_cell], f1_send.at[j], f1_recv.at[j], cell_at(j))
        for j in range(1, n_cell)
    ]

    def chunks(some):
        for at in some:
            if at + part < n_faces:
                build(at + part, part)
            gather(at, part)

    joined = early + (len(starts) - early) // 2
    chunks(starts[early:joined])
    for copy in first:
        copy.wait_recv()
    summed = forces_1[0]
    for j in range(1, n_cell):
        summed = summed + forces_1[j]
    forces_2[0] = summed
    chunks(starts[joined : joined + 1])
    second = [
        send(forces_2.at[0], forces_2.at[j], f2_send.at[j], f2_recv.at[j], circ_at(j))
        for j in range(1, n_circ)
    ]
    chunks(starts[joined + 1 :])
    shapes = mode_shapes[...].reshape(2 * walls_k * n_circ, mode_shapes.shape[3])
    by_passage = jnp.dot(modes_c[...], shapes, precision=HI, preferred_element_type=F32)

    total[...] = lax.dot_general(
        flux[...], tiles(signed, 0, n_faces), NT, preferred_element_type=F32
    )

    to_below.wait_recv()
    to_above.wait_recv()
    stack[0:padded, :] = u
    above_rows = above[...].astype(F32)
    stack[padded : padded + side_rows, :] = jnp.where(
        me_cell == n_cell - 1, 0.0, above_rows
    ).astype(BF16)
    below_rows = below[0:side_rows, :].astype(F32)
    stack[padded + side_rows :, :] = jnp.where(
        me_cell == 0, -cell_out[0:side_rows, :].astype(F32), below_rows
    ).astype(BF16)
    below_damp = below[side_rows : side_rows + 16, :].astype(F32)[0:1]
    below_damp = jnp.where(me_cell == 0, 0.0, below_damp)
    held = stack[...]
    derived = dot(fixed_c[...], held)
    result = by_layer(derived[0:padded], pattern_of(time_coef[0] * (1.0 / scale)))
    result = result - by_layer(derived[padded : 2 * padded], pattern_of(0.5 * damp))
    lower_damp = jnp.concatenate([below_damp, damp[0 : layers - 1]], axis=0)
    result = result - by_layer(derived[2 * padded :], pattern_of(0.5 * lower_damp))
    result = result + dot(axial_mix, held)

    to_prev.wait_recv()
    to_next.wait_recv()
    left = lax.broadcasted_iota(jnp.int32, (padded, 2 * per), 1) < per
    ahead = pltpu.roll(side_next[0:padded, :].astype(F32), per, 1)
    back = pltpu.roll(side_prev[0:padded, :].astype(F32), per, 1)
    back_damp = side_prev[padded:, :].astype(F32)[0:8]
    lower = jnp.where(left, own_side, back)
    upper = jnp.where(left, ahead, own_side)
    side_s = 0.5 * jnp.where(left[0:8], side_pattern, back_damp)
    lower_b, upper_b = lower.astype(BF16), upper.astype(BF16)
    side_flux = dot(side_mix, lower_b) + dot(side_mix, upper_b)
    side_flux = side_flux - by_layer(upper - lower, side_s)
    side_flux = jnp.where(left, side_flux, -side_flux).astype(BF16)
    result = result + lax.dot_general(
        side_flux, tiles(extra, n_walls, 2 * per), NT, preferred_element_type=F32
    )
    result = result + total[...]
    for r in range(n_rows):
        image[r] = result[r * layers : (r + 1) * layers].astype(BF16)

    for copy in second:
        copy.wait_recv()
    every = forces_2[0]
    for j in range(1, n_circ):
        every = every + forces_2[j]
    answer = jnp.dot(every, by_passage, precision=HI, preferred_element_type=F32)
    modal[...] = answer[0:HB]
    for copy in copies:
        copy.wait_send()


def deliver(image, modal, image_out, modal_out, sems):
    copies = [
        pltpu.make_async_copy(image, image_out, sems.at[0]),
        pltpu.make_async_copy(modal, modal_out, sems.at[1]),
    ]
    for copy in copies:
        copy.start()
    for copy in copies:
        copy.wait()


def shards(
    flow_state, time_coef, axial_damp, plane_damp, periodic_damp, flux_jacobian, face_cells,
    periodic_cells, face_map, wall_cells, wall_normals, pressure_weights, mode_shapes,
):
    layers, cells = flow_state.shape[2:]
    n_cell = lax.axis_size("cell")
    n_circ = lax.axis_size("circ")
    walls_k = wall_normals.shape[0]
    n_modes = mode_shapes.shape[3]
    per = face_map.shape[0]
    n_faces = face_cells.shape[1]
    n_walls = wall_cells.shape[0]
    fixed, scale = constants(layers, n_circ, walls_k)
    padded = fixed[0].shape[0]
    side = fixed[3].shape[0] // 2
    lanes = fixed[7].shape[0]
    state = flow_state.reshape(HB * NV, layers, cells)
    vmem = pl.BlockSpec(memory_space=pltpu.VMEM)
    smem = pl.BlockSpec(memory_space=pltpu.SMEM)
    dma = pltpu.SemaphoreType.DMA
    image, modal = pl.pallas_call(
        functools.partial(
            kernel, n_cell=n_cell, n_circ=n_circ, layers=layers, padded=padded, scale=scale
        ),
        out_shape=(
            jax.ShapeDtypeStruct((HB * NV, layers, cells), BF16),
            jax.ShapeDtypeStruct((HB, n_modes), F32),
        ),
        in_specs=[vmem] * 11 + [smem] + [vmem] * 9,
        out_specs=(vmem, vmem),
        scratch_shapes=[
            pltpu.VMEM(((n_walls + 2 * per) // 128, cells, 128), BF16),
            pltpu.VMEM((n_faces // 128, cells, 128), BF16),
            pltpu.VMEM((padded + 2 * side, cells), BF16),
            pltpu.VMEM((2 * side + 16, cells), BF16),
            pltpu.VMEM((side, cells), BF16),
            pltpu.VMEM((side + 16, cells), BF16),
            pltpu.VMEM((padded + 16, 2 * per), BF16),
            pltpu.VMEM((padded + 16, 2 * per), BF16),
            pltpu.VMEM((padded + 16, 2 * per), BF16),
            pltpu.VMEM((n_cell, 8, lanes), F32),
            pltpu.VMEM((n_circ, 8, lanes), F32),
            pltpu.VMEM((padded, n_faces), BF16),
            pltpu.VMEM((padded, cells), F32),
            dma((2,)), dma((2,)), dma((2,)), dma((2,)),
            dma((n_cell,)), dma((n_cell,)), dma((n_circ,)), dma((n_circ,)),
        ],
        compiler_params=pltpu.CompilerParams(collective_id=0, has_side_effects=True),
    )(
        state, time_coef, axial_damp, plane_damp, periodic_damp,
        flux_jacobian.transpose(1, 0, 2), face_cells, periodic_cells, face_map[None], wall_cells[None], wall_normals, pressure_weights,
        mode_shapes.transpose(0, 2, 1, 3), *fixed,
    )
    anywhere = pl.BlockSpec(memory_space=pl.ANY)
    image, modal = pl.pallas_call(
        deliver,
        out_shape=(
            jax.ShapeDtypeStruct(image.shape, BF16),
            jax.ShapeDtypeStruct(modal.shape, F32),
        ),
        in_specs=[anywhere] * 2,
        out_specs=(vmem, vmem),
        scratch_shapes=[dma((2,))],
    )(image, modal)
    return image.reshape(HB * NV, 1, layers, cells), modal


def solution(mesh):
    circ = P("circ", "cell", None)
    placed = (
        P(None, "circ", "cell", None), circ, circ, circ, circ, P(), P(), P(), P(),
        P("cell"), P(None, "cell"), P(), P(),
    )
    return jax.shard_map(
        shards,
        mesh=mesh,
        in_specs=placed,
        out_specs=(P(None, "circ", "cell", None), P()),
        check_vma=False,
    )
```
